256 devices in a mesh: ctx: 32 (over z, y_lo, core), head: 8 (over x, y_hi).
Axes of the slice: x: 4, y: 4 (y_hi: 2, y_lo: 2; y = y_hi * 2 + y_lo), z: 8, core: 2. Of those that a mesh axis runs over, the one named last changes fastest.
Arguments:
- query: bfloat16 [4096, 8192], P('ctx', 'head'), may hold values from -11 to 11
- key_in: bfloat16 [4096, 1024], P('ctx', 'head'), may hold values from -11 to 11
- value: bfloat16 [4096, 1024], P('ctx', 'head'), may hold values from -6 to 6
- grad_y: bfloat16 [4096, 8192], P('ctx', 'head'), may hold values from -6 to 6
- w_out: bfloat16 [8192, 8192], P('head', 'ctx'), may hold values from -0.0625 to 0.0625
- parent: int32 [32], replicated, may hold values from 1 to 31, as said below
Outputs:
- grad_query: bfloat16 [4096, 8192], P('ctx', 'head')
- grad_key: bfloat16 [4096, 1024], P('ctx', 'head')
- grad_value: bfloat16 [4096, 1024], P('ctx', 'head')
The draws below stay inside these ranges and needn't reach their ends.
Inputs may be any that keep to these rules, and one draw needn't show every extreme that they name: The shared prefix is blocks 32 - 4 to 31: parent[31] = 31 and parent[b] = b + 1 for the other prefix blocks; the earlier blocks form particles of 4 consecutive blocks, in which each block's parent is the block after it, except a particle's last block, whose parent is a block of the shared prefix.
All inputs are finite; a program needn't handle non-finite values.
Results may differ from the reference program's by a relative error of at most 0.014.
Values may be sent and summed in bfloat16 or wider, within the bound.
A program may use at most 128 MiB of HBM per device.

```python
import jax
import jax.numpy as jnp
from jax import lax

D = 8192
H_KV = 8
HPG = 8
DH = 128
BLOCK = 128
PREFIX = 4
PARTICLE = 4
TOKENS = 4096
NBLOCKS = 32
HEADS = 64


def paired_draw(key):
    base = jax.random.fold_in(key, 11)
    query_key, key_key = jax.random.split(base, 2)
    heads = H_KV * HPG
    queries = jnp.clip(jax.random.normal(query_key, (TOKENS, heads * DH), jnp.float32), -6.0, 6.0)
    keys = jnp.clip(jax.random.normal(key_key, (TOKENS, H_KV * DH), jnp.float32), -6.0, 6.0)
    return (queries.astype(jnp.bfloat16), keys.astype(jnp.bfloat16))


def draw_query(key, part):
    return paired_draw(key)[0]


def draw_key_in(key, part):
    return paired_draw(key)[1]


def draw_parent(key, part):
    blocks = jnp.arange(NBLOCKS, dtype=jnp.int32)
    first_prefix = NBLOCKS - PREFIX
    roots = jax.random.randint(jax.random.fold_in(key, 3), (NBLOCKS,), first_prefix, NBLOCKS, dtype=jnp.int32)
    trailing = (blocks < first_prefix) & (blocks % PARTICLE == PARTICLE - 1)
    return jnp.where(trailing, roots, jnp.minimum(blocks + 1, NBLOCKS - 1)).astype(jnp.int32)


def level_of(rng, dims, cuts, smallest, largest):
    level = 1.0
    for axis_at, parts in cuts:
        draws = jax.random.uniform(jax.random.fold_in(jax.random.fold_in(rng, 6), axis_at), (parts,), jnp.float32, smallest / len(cuts), largest / len(cuts))
        level = level * jnp.repeat(jnp.exp(draws), dims[axis_at] // parts).reshape((-1,) + (1,) * (len(dims) - 1 - axis_at))
    return level


def scatter_about(key, shape, scale, limit, cuts=(), held_as=jnp.bfloat16):
    factor_of = level_of(key, shape, cuts, -0.22, 0.18) if cuts else 1.0
    result = jax.random.normal(key, shape, jnp.float32) * scale * factor_of
    return jnp.minimum(jnp.maximum(result, -limit), limit).astype(held_as)


def setup_inputs(seed: int = 0) -> dict:
    key_of = jax.random.split(jax.random.key(seed), 7)
    return {
        "query": draw_query(jax.random.fold_in(key_of[6], 71), 0),
        "key_in": draw_key_in(jax.random.fold_in(key_of[6], 71), 0),
        "value": scatter_about(key_of[2], (TOKENS, H_KV * DH), 1.0, 6.0, ((0, 32), (1, 8))),
        "grad_y": scatter_about(key_of[3], (TOKENS, D), 1.0, 6.0, ((0, 32), (1, 8))),
        "w_out": scatter_about(key_of[4], (HEADS * DH, D), (HEADS * DH) ** -0.5, 0.0625, ((0, 8), (1, 32))),
        "parent": draw_parent(jax.random.fold_in(key_of[6], 71), 0),
    }


def ancestors(parent):
    count = parent.shape[0]
    index = jnp.arange(count, dtype=jnp.int32)
    start = (index[:, None] == index[None, :]).astype(jnp.int32)

    def advance(step, state):
        current, marks = state
        current = jnp.sum(jnp.where(current[:, None] == index[None, :], parent[None, :], 0), axis=1).astype(jnp.int32)
        marks = jnp.maximum(marks, (current[:, None] == index[None, :]).astype(jnp.int32))
        return current, marks

    return lax.fori_loop(0, count, advance, (index, start))[1]


def reference(query, key_in, value, grad_y, w_out, parent):
    total = query.shape[0]
    scale = DH ** -0.5
    grad_attn = lax.dot_general(grad_y, w_out, (((1,), (1,)), ((), ())), preferred_element_type=jnp.float32).astype(jnp.bfloat16)
    visible = ancestors(parent)
    position = jnp.arange(total, dtype=jnp.int32)
    block_of = position // BLOCK
    allowed = (visible[block_of][:, block_of] > 0) & ((block_of[:, None] != block_of[None, :]) | (position[None, :] <= position[:, None]))
    query_heads = query.reshape(total, H_KV, HPG, DH).transpose(1, 2, 0, 3)
    grad_heads = grad_attn.reshape(total, H_KV, HPG, DH).transpose(1, 2, 0, 3)
    key_heads = key_in.reshape(total, H_KV, DH).transpose(1, 0, 2)
    value_heads = value.reshape(total, H_KV, DH).transpose(1, 0, 2)

    def group(items):
        query_group, grad_group, key_group, value_group = items

        def one_head(carry, pair):
            key_sum, value_sum = carry
            query_one, grad_one = pair
            scores = jnp.dot(query_one, key_group.T, preferred_element_type=jnp.float32) * scale
            masked = jnp.where(allowed, scores, -1e30)
            top = jnp.max(masked, axis=1)
            weights = jnp.where(allowed, jnp.exp(scores - top[:, None]), 0.0)
            prob = weights / jnp.sum(weights, axis=1)[:, None]
            dprob = jnp.dot(grad_one, value_group.T, preferred_element_type=jnp.float32)
            delta = jnp.sum(prob * dprob, axis=1)
            prob_low = prob.astype(jnp.bfloat16)
            value_sum = value_sum + jnp.dot(prob_low.T, grad_one, preferred_element_type=jnp.float32)
            dscore = (prob * (dprob - delta[:, None])).astype(jnp.bfloat16)
            grad_q = jnp.dot(dscore, key_group, preferred_element_type=jnp.float32) * scale
            key_sum = key_sum + jnp.dot(dscore.T, query_one, preferred_element_type=jnp.float32) * scale
            return (key_sum, value_sum), grad_q

        empty = jnp.zeros((total, DH), jnp.float32)
        (key_sum, value_sum), grad_q = lax.scan(one_head, (empty, empty), (query_group, grad_group))
        return grad_q, key_sum, value_sum

    grad_q, grad_k, grad_v = lax.map(group, (query_heads, grad_heads, key_heads, value_heads))
    grad_query = grad_q.transpose(2, 0, 1, 3).reshape(total, H_KV * HPG * DH).astype(jnp.bfloat16)
    grad_key = grad_k.transpose(1, 0, 2).reshape(total, H_KV * DH).astype(jnp.bfloat16)
    grad_value = grad_v.transpose(1, 0, 2).reshape(total, H_KV * DH).astype(jnp.bfloat16)
    return (grad_query, grad_key, grad_value)
```

```python
import functools

import jax
import jax.numpy as jnp
from jax import lax
from jax.experimental import pallas as pl
from jax.experimental.pallas import tpu as pltpu
from jax.sharding import PartitionSpec as P

DH = 128
HPG = 8
GROUP = 4
NZ = 8
NH = 8
ROWS = 16
BF16 = jnp.bfloat16
F32 = jnp.float32
MESH = pl.DeviceIdType.MESH


def dot_nt(a, b):
    return lax.dot_general(a, b, (((1,), (1,)), ((), ())), preferred_element_type=F32)


def dot_nn(a, b):
    return lax.dot_general(a, b, (((1,), (0,)), ((), ())), preferred_element_type=F32)


def kernel(
    q_hbm, k_hbm, v_hbm, g_hbm, w_hbm, parent_ref,
    dq_ref, dk_ref, dv_ref,
    q_v, kv, s1, a, bw, cb, sp, rp, ga, gat, qt, bias, pf, plow, ds, dt, dsend, r1, psend, r2, fin,
    loc, p1s, p1r, p2s, p2r, ags, agr, bs, br, kvs, kvr, pxs, pxr, rss, rsr, d1s, d1r, d2s, d2r,
):
    ctx = lax.axis_index("ctx")
    head = lax.axis_index("head")
    z = ctx // GROUP
    m = ctx % GROUP
    x = head // 2
    yh = head % 2
    scale = DH ** (-0.5)
    sends = []

    def at_head(h):
        return (ctx, h)

    def at_z(zz):
        return (zz * GROUP + m, head)

    def at_m(mm):
        return (z * GROUP + mm, head)

    def remote(src, dst, send_sem, recv_sem, device):
        return pltpu.make_async_remote_copy(
            src_ref=src, dst_ref=dst, send_sem=send_sem, recv_sem=recv_sem,
            device_id=device, device_id_type=MESH,
        )

    def send(src, dst, send_sem, recv_sem, device):
        copy = remote(src, dst, send_sem, recv_sem, device)
        copy.start()
        sends.append(copy)

    def arrived(dst, recv_sem, device):
        remote(dst, dst, loc.at[0], recv_sem, device).wait_recv()

    local = [
        pltpu.make_async_copy(k_hbm, kv.at[0, 2 * m], loc.at[0]),
        pltpu.make_async_copy(v_hbm, kv.at[1, 2 * m], loc.at[1]),
        pltpu.make_async_copy(g_hbm.at[pl.ds(head * ROWS, ROWS)], s1.at[head], loc.at[2]),
        pltpu.make_async_copy(q_hbm, q_v, loc.at[3]),
        pltpu.make_async_copy(w_hbm, bw.at[m], loc.at[4]),
    ]
    for copy in local:
        copy.start()

    barrier = pltpu.get_barrier_semaphore()
    for i in range(1, NH):
        pl.semaphore_signal(barrier, inc=1, device_id=at_head((head + i) % NH), device_id_type=MESH)
    for i in range(1, NZ):
        pl.semaphore_signal(barrier, inc=1, device_id=at_z((z + i) % NZ), device_id_type=MESH)
    for i in range(1, GROUP):
        pl.semaphore_signal(barrier, inc=1, device_id=at_m((m + i) % GROUP), device_id_type=MESH)
    pl.semaphore_wait(barrier, NH + NZ + GROUP - 3)

    core_mate = at_m(m + 1 - 2 * (m % 2))
    m_core = m + 1 - 2 * (m % 2)
    m_side = (m + 2) % GROUP
    m_far = (m_core + 2) % GROUP

    for i in range(1, NH):
        h = (head + i) % NH
        send(g_hbm.at[pl.ds(h * ROWS, ROWS)], s1.at[head], p1s.at[i], p1r.at[head], at_head(h))

    @pl.when(z == NZ - 1)
    def _():
        for i in range(NZ - 1):
            remote(k_hbm, kv.at[0, 2 * m + 1], pxs.at[0, i], pxr.at[0], at_z(i)).start()
            remote(v_hbm, kv.at[1, 2 * m + 1], pxs.at[1, i], pxr.at[1], at_z(i)).start()

    local[0].wait()
    local[1].wait()
    for i in range(1, GROUP):
        mm = (m + i) % GROUP
        for c in range(2):
            send(kv.at[c, 2 * m], kv.at[c, 2 * m], kvs.at[c, 0, i], kvr.at[c, 2 * m], at_m(mm))
    half = w_hbm.shape[0] // 2
    for r in range(2):
        part = pl.ds(r * half, half)
        if r == 0:
            send(w_hbm.at[part], bw.at[m, part], bs.at[0, r], br.at[m, r], at_m(m_side))
        send(w_hbm.at[part], bw.at[m, part], bs.at[1, r], br.at[m, r], core_mate)

    for i in range(NH):
        k = (head + i) % NH
        if i == 0:
            local[2].wait()
        else:
            arrived(s1.at[k], p1r.at[k], at_head(k))

        @pl.when(k == z)
        def _():
            pltpu.make_async_copy(s1.at[k], a.at[head, z], loc.at[5]).start()

        @pl.when(k != z)
        def _():
            remote(s1.at[k], a.at[head, z], p2s.at[k], p2r.at[z], at_z(k)).start()

    @pl.when(z == NZ - 1)
    def _():
        for c in range(2):
            pltpu.make_async_copy(kv.at[c, 2 * m], kv.at[c, 2 * m + 1], loc.at[6 + c]).start()
        for c in range(2):
            pltpu.make_async_copy(kv.at[c, 2 * m], kv.at[c, 2 * m + 1], loc.at[6 + c]).wait()

    @pl.when(z != NZ - 1)
    def _():
        for c in range(2):
            arrived(kv.at[c, 2 * m + 1], pxr.at[c], at_z(0))

    for i in range(1, GROUP):
        mm = (m + i) % GROUP
        for c in range(2):
            send(kv.at[c, 2 * m + 1], kv.at[c, 2 * m + 1], kvs.at[c, 1, i], kvr.at[c, 2 * m + 1], at_m(mm))
    part = pl.ds(half, half)
    send(w_hbm.at[part], bw.at[m, part], bs.at[0, 1], br.at[m, 1], at_m(m_side))

    shape = bias.shape
    row = lax.broadcasted_iota(jnp.int32, shape, 0)
    col = lax.broadcasted_iota(jnp.int32, shape, 1)
    key_block = col // (2 * DH)
    in_prefix = (col // DH) % 2
    within = col % DH
    own_kind = jnp.where(z == NZ - 1, 1, 0)
    root = jnp.where(z == NZ - 1, GROUP, parent_ref[z * GROUP + GROUP - 1] - (NZ - 1) * GROUP)
    own_part = (in_prefix == own_kind) & (
        (key_block > m) | ((key_block == m) & (within <= row))
    )
    allowed = own_part | ((in_prefix == 1) & (key_block >= root))
    bias[...] = jnp.where(allowed, 0.0, -1e30)
    local[3].wait()
    for h in range(HPG):
        cols = pl.ds(h * DH, DH)
        qt[:, cols] = q_v[:, cols].astype(F32).T.astype(BF16)

    for i in range(1, NZ):
        zz = (z + i) % NZ
        arrived(a.at[head, zz], p2r.at[zz], at_z(zz))
    pltpu.make_async_copy(s1.at[0], a.at[head, z], loc.at[5]).wait()

    def x_at(dx):
        return 2 * ((x + dx) % 4) + yh

    h_y = 2 * x + 1 - yh
    send(a.at[head], a.at[head], ags.at[0], agr.at[head], at_head(x_at(1)))
    send(a.at[head], a.at[head], ags.at[1], agr.at[head], at_head(x_at(3)))
    send(a.at[head], a.at[head], ags.at[2], agr.at[head], at_head(h_y))
    send(a.at[head], a.at[head], ags.at[3], agr.at[head], at_head(x_at(2)))

    for c in range(2):
        for i in range(1, GROUP):
            mm = (m + i) % GROUP
            for t in range(2):
                arrived(kv.at[c, 2 * mm + t], kvr.at[c, 2 * mm + t], at_m(mm))

    def forward_head(h, carry):
        cols = pl.ds(pl.multiple_of(h * DH, DH), DH)
        keys = kv[0].reshape(2 * GROUP * DH, DH)
        s = dot_nt(q_v[:, cols], keys) * scale + bias[...]
        w = jnp.exp(s - jnp.max(s, axis=1, keepdims=True))
        p = w * (1.0 / jnp.sum(w, axis=1, keepdims=True))
        pf[cols, :] = p
        plow[cols, :] = p.astype(BF16)
        return carry

    lax.fori_loop(0, HPG // 2, forward_head, 0)

    for r in range(2):
        part = pl.ds(r * half, half)
        arrived(bw.at[m_side, part], br.at[m_side, r], core_mate)
        send(bw.at[m_side, part], bw.at[m_side, part], bs.at[2, r], br.at[m_side, r], core_mate)

    lax.fori_loop(HPG // 2, HPG, forward_head, 0)

    local[4].wait()
    for r in range(2):
        part = pl.ds(r * half, half)
        arrived(bw.at[m_core, part], br.at[m_core, r], core_mate)
        arrived(bw.at[m_far, part], br.at[m_far, r], core_mate)

    up = at_z((z + 1) % NZ)
    down = at_z((z + NZ - 1) % NZ)
    width = s1.shape[2]
    steps = NZ // 2
    side = (pl.ds(0, width // 2), pl.ds(width // 2, width // 2))

    def head_of(j):
        dx = 0
        dy = 0
        for at, (vx, vy) in enumerate([(0, 0), (1, 0), (3, 0), (0, 1), (2, 0), (1, 1), (3, 1), (2, 1)]):
            hit = jnp.where(j == at, 1, 0)
            dx = dx + vx * hit
            dy = dy + vy * hit
        return 2 * ((x + dx) % 4) + (yh + dy) % 2

    def hop(j, d, s):
        where = (slice(None), side[d]) if s == 0 else (slice(None), slice(None))
        return remote(
            sp.at[(j, d, s) + where], rp.at[(j, d, s) + where], rss.at[j, d, s], rsr.at[j, d, s],
            up if d == 0 else down,
        )

    def slot(t, carry):
        for s in range(steps, 0, -1):
            j = t - s

            @pl.when((j >= 0) & (j < NH))
            def _():
                for d in range(2):
                    hop(j, d, s - 1).wait_recv()
                    if s < steps:
                        dest = (z + steps - s) % NZ if d == 0 else (z + steps + s) % NZ
                        mine = pl.ds(pl.multiple_of(dest * ROWS, ROWS), ROWS)
                        if s == 1:
                            other = side[1 - d]
                            sp[j, d, s, :, side[d]] = (
                                cb[j, mine, side[d]] + rp[j, d, 0, :, side[d]].astype(F32)
                            ).astype(BF16)
                            sp[j, d, s, :, other] = cb[j, mine, other].astype(BF16)
                        else:
                            sp[j, d, s] = (cb[j, mine, :] + rp[j, d, s - 1].astype(F32)).astype(BF16)
                        hop(j, d, s).start()
                if s == steps:
                    mine = pl.ds(pl.multiple_of(z * ROWS, ROWS), ROWS)
                    total = cb[j, mine, :] + rp[j, 0, s - 1].astype(F32) + rp[j, 1, s - 1].astype(F32)
                    place = pl.multiple_of(head_of(j) * ROWS, ROWS)
                    ga[pl.ds(place, ROWS), :] = total.astype(BF16)

        @pl.when(t < NH)
        def _():
            h = head_of(t)

            @pl.when(t > 0)
            def _():
                arrived(a.at[h], agr.at[h], at_head(h_y))

            @pl.when(t == 3)
            def _():
                remote(a.at[h], a.at[h], ags.at[4], agr.at[h], at_head(x_at(1))).start()
                remote(a.at[h], a.at[h], ags.at[5], agr.at[h], at_head(x_at(3))).start()

            @pl.when(t == 4)
            def _():
                remote(a.at[h], a.at[h], ags.at[6], agr.at[h], at_head(h_y)).start()

            wide = bw.shape[2]
            for n in range(width // wide):
                cols = pl.ds(n * wide, wide)
                acc = None
                for b in range(GROUP):
                    rows = a[h, :, :, pl.ds(b * wide, wide)].reshape(NZ * ROWS, wide)
                    term = dot_nt(rows, bw[b, cols, :])
                    acc = term if acc is None else acc + term
                cb[t, :, cols] = acc
            far = pl.ds(pl.multiple_of(((z + steps) % NZ) * ROWS, ROWS), ROWS)
            for d in range(2):
                sp[t, d, 0, :, side[d]] = cb[t, far, side[d]].astype(BF16)
                hop(t, d, 0).start()

        return carry

    lax.fori_loop(0, NH + steps, slot, 0)

    mates = [(m + i) % GROUP for i in range(1, GROUP)]

    def spread(c, scaled):
        for b in range(2 * GROUP):
            dsend[c, b] = (dt[c, :, pl.ds(b * DH, DH)] * scaled).astype(BF16)
        for i, mm in enumerate(mates):
            pair = pl.ds(2 * mm, 2)
            send(dsend.at[c, pair], r1.at[c, m], d1s.at[c, i], d1r.at[c, m], at_m(mm))

    for h in range(HPG):
        cols = pl.ds(h * DH, DH)
        gat[:, cols] = ga[:, cols].astype(F32).T.astype(BF16)
    dt[0] = dot_nn(gat[...], plow[...])
    spread(0, 1.0)

    def backward_head(h, carry):
        cols = pl.ds(pl.multiple_of(h * DH, DH), DH)
        values = kv[1].reshape(2 * GROUP * DH, DH)
        dprob = dot_nt(ga[:, cols], values)
        p = pf[cols, :]
        delta = jnp.sum(p * dprob, axis=1, keepdims=True)
        ds[cols, :] = (p * (dprob - delta)).astype(BF16)
        return carry

    lax.fori_loop(0, HPG, backward_head, 0)
    dt[1] = dot_nn(qt[...], ds[...])
    spread(1, scale)

    def query_head(h, carry):
        cols = pl.ds(pl.multiple_of(h * DH, DH), DH)
        keys = kv[0].reshape(2 * GROUP * DH, DH)
        dq_ref[:, cols] = (dot_nn(ds[cols, :], keys) * scale).astype(BF16)
        return carry

    lax.fori_loop(0, HPG, query_head, 0)

    last = at_z(NZ - 1)
    for c in range(2):
        scaled = scale if c else 1.0
        for t in range(2):
            cols = pl.ds(pl.multiple_of((2 * m + t) * DH, DH), DH)
            fin[c, t] = dt[c, :, cols] * scaled
        for mm in mates:
            arrived(r1.at[c, mm], d1r.at[c, mm], at_m(mm))
            for t in range(2):
                fin[c, t] = fin[c, t] + r1[c, mm, t].astype(F32)

        @pl.when(z != NZ - 1)
        def _():
            psend[c] = fin[c, 1].astype(BF16)
            remote(psend.at[c], r2.at[c, z], d2s.at[c], d2r.at[c, z], last).start()

    for c in range(2):
        @pl.when(z == NZ - 1)
        def _():
            fin[c, 0] = fin[c, 0] + fin[c, 1]
            for zz in range(NZ - 1):
                arrived(r2.at[c, zz], d2r.at[c, zz], at_z(zz))
                fin[c, 0] = fin[c, 0] + r2[c, zz].astype(F32)

        out = dk_ref if c else dv_ref
        out[...] = fin[c, 0].T.astype(BF16)

    for copy in sends:
        copy.wait_send()
    for k in range(NH):
        @pl.when(k != z)
        def _():
            remote(s1.at[k], a.at[head, z], p2s.at[k], p2r.at[z], up).wait_send()

    for i in range(4, 7):
        remote(a.at[head], a.at[head], ags.at[i], agr.at[head], up).wait_send()

    @pl.when(z == NZ - 1)
    def _():
        for i in range(NZ - 1):
            remote(k_hbm, kv.at[0, 2 * m + 1], pxs.at[0, i], pxr.at[0], up).wait_send()
            remote(v_hbm, kv.at[1, 2 * m + 1], pxs.at[1, i], pxr.at[1], up).wait_send()

    @pl.when(z != NZ - 1)
    def _():
        for c in range(2):
            remote(psend.at[c], r2.at[c, z], d2s.at[c], d2r.at[c, z], up).wait_send()

    def drain(j, carry):
        for d in range(2):
            for s in range(steps):
                hop(j, d, s).wait_send()
        return carry

    lax.fori_loop(0, NH, drain, 0)


def per_device(query, key_in, value, grad_y, w_out, parent):
    tokens, width = query.shape
    keys = 2 * GROUP * DH
    dma = pltpu.SemaphoreType.DMA
    anywhere = pl.BlockSpec(memory_space=pl.ANY)
    vmem = pl.BlockSpec(memory_space=pltpu.VMEM)
    return pl.pallas_call(
        kernel,
        out_shape=(
            jax.ShapeDtypeStruct(query.shape, BF16),
            jax.ShapeDtypeStruct(key_in.shape, BF16),
            jax.ShapeDtypeStruct(value.shape, BF16),
        ),
        in_specs=[anywhere] * 5 + [pl.BlockSpec(memory_space=pltpu.SMEM)],
        out_specs=(vmem, vmem, vmem),
        scratch_shapes=[
            pltpu.VMEM((tokens, width), BF16),
            pltpu.VMEM((2, 2 * GROUP, DH, DH), BF16),
            pltpu.VMEM((NH, ROWS, width), BF16),
            pltpu.VMEM((NH, NZ, ROWS, width), BF16),
            pltpu.VMEM((GROUP,) + w_out.shape, BF16),
            pltpu.VMEM((NH, tokens, width), F32),
            pltpu.VMEM((NH, 2, NZ // 2, ROWS, width), BF16),
            pltpu.VMEM((NH, 2, NZ // 2, ROWS, width), BF16),
            pltpu.VMEM((tokens, width), BF16),
            pltpu.VMEM((tokens, width), BF16),
            pltpu.VMEM((tokens, width), BF16),
            pltpu.VMEM((tokens, keys), F32),
            pltpu.VMEM((width, keys), F32),
            pltpu.VMEM((width, keys), BF16),
            pltpu.VMEM((width, keys), BF16),
            pltpu.VMEM((2, DH, keys), F32),
            pltpu.VMEM((2, 2 * GROUP, DH, DH), BF16),
            pltpu.VMEM((2, GROUP, 2, DH, DH), BF16),
            pltpu.VMEM((2, DH, DH), BF16),
            pltpu.VMEM((2, NZ, DH, DH), BF16),
            pltpu.VMEM((2, 2, DH, DH), F32),
            dma((8,)),
            dma((NH,)), dma((NH,)),
            dma((NH,)), dma((NZ,)),
            dma((7,)), dma((NH,)),
            dma((3, 2)), dma((GROUP, 2)),
            dma((2, 2, GROUP)), dma((2, 2 * GROUP)),
            dma((2, NZ)), dma((2,)),
            dma((NH, 2, NZ // 2)), dma((NH, 2, NZ // 2)),
            dma((2, GROUP)), dma((2, GROUP)),
            dma((2,)), dma((2, NZ)),
        ],
        compiler_params=pltpu.CompilerParams(
            collective_id=0, has_side_effects=True, vmem_limit_bytes=60 * 1024 * 1024
        ),
        name="tree_attention_backward",
    )(query, key_in, value, grad_y, w_out, parent)


def solution(mesh):
    placed = (
        P("ctx", "head"),
        P("ctx", "head"),
        P("ctx", "head"),
        P("ctx", "head"),
        P("head", "ctx"),
        P(),
    )
    return jax.shard_map(
        per_device,
        mesh=mesh,
        in_specs=placed,
        out_specs=(P("ctx", "head"), P("ctx", "head"), P("ctx", "head")),
        check_vma=False,
    )
```

```python
import functools

import jax
import jax.numpy as jnp
from jax import lax
from jax.experimental import pallas as pl
from jax.experimental.pallas import tpu as pltpu
from jax.sharding import PartitionSpec as P

DH = 128
HPG = 8
GROUP = 4
NZ = 8
NH = 8
ROWS = 16
SKEW = 2
BF16 = jnp.bfloat16
F32 = jnp.float32
MESH = pl.DeviceIdType.MESH


def dot_nt(a, b):
    return lax.dot_general(a, b, (((1,), (1,)), ((), ())), preferred_element_type=F32)


def dot_nn(a, b):
    return lax.dot_general(a, b, (((1,), (0,)), ((), ())), preferred_element_type=F32)


def kernel(
    q_hbm, k_hbm, v_hbm, g_hbm, w_hbm, parent_ref,
    dq_ref, dk_ref, dv_ref,
    q_v, kv, s1, a, bw, cb, sp, rp, ga, gat, qt, bias, pf, plow, ds, dt, dsend, r1, psend, r2, fin,
    loc, p1s, p1r, p2s, p2r, ags, agr, bs, br, kvs, kvr, pxs, pxr, rss, rsr, d1s, d1r, d2s, d2r,
):
    ctx = lax.axis_index("ctx")
    head = lax.axis_index("head")
    z = ctx // GROUP
    m = ctx % GROUP
    x = head // 2
    yh = head % 2
    scale = DH ** (-0.5)
    sends = []

    def at_head(h):
        return (ctx, h)

    def at_z(zz):
        return (zz * GROUP + m, head)

    def at_m(mm):
        return (z * GROUP + mm, head)

    def remote(src, dst, send_sem, recv_sem, device):
        return pltpu.make_async_remote_copy(
            src_ref=src, dst_ref=dst, send_sem=send_sem, recv_sem=recv_sem,
            device_id=device, device_id_type=MESH,
        )

    def send(src, dst, send_sem, recv_sem, device):
        copy = remote(src, dst, send_sem, recv_sem, device)
        copy.start()
        sends.append(copy)

    def arrived(dst, recv_sem, device):
        remote(dst, dst, loc.at[0], recv_sem, device).wait_recv()

    local = [
        pltpu.make_async_copy(k_hbm, kv.at[0, 2 * m], loc.at[0]),
        pltpu.make_async_copy(v_hbm, kv.at[1, 2 * m], loc.at[1]),
        pltpu.make_async_copy(g_hbm.at[pl.ds(head * ROWS, ROWS)], s1.at[head], loc.at[2]),
        pltpu.make_async_copy(q_hbm, q_v, loc.at[3]),
        pltpu.make_async_copy(w_hbm, bw.at[m], loc.at[4]),
    ]
    for copy in local:
        copy.start()

    barrier = pltpu.get_barrier_semaphore()
    for i in range(1, NH):
        pl.semaphore_signal(barrier, inc=1, device_id=at_head((head + i) % NH), device_id_type=MESH)
    for i in range(1, NZ):
        pl.semaphore_signal(barrier, inc=1, device_id=at_z((z + i) % NZ), device_id_type=MESH)
    for i in range(1, GROUP):
        pl.semaphore_signal(barrier, inc=1, device_id=at_m((m + i) % GROUP), device_id_type=MESH)
    pl.semaphore_wait(barrier, NH + NZ + GROUP - 3)

    core_mate = at_m(m + 1 - 2 * (m % 2))
    m_core = m + 1 - 2 * (m % 2)
    m_side = (m + 2) % GROUP
    m_far = (m_core + 2) % GROUP

    for i in range(1, NH):
        h = (head + i) % NH
        send(g_hbm.at[pl.ds(h * ROWS, ROWS)], s1.at[head], p1s.at[i], p1r.at[head], at_head(h))

    half = w_hbm.shape[0] // 2
    for r in range(2):
        part = pl.ds(r * half, half)
        send(w_hbm.at[part], bw.at[m, part], bs.at[0, r], br.at[m, r], at_m(m_side))
    for r in range(2):
        part = pl.ds(r * half, half)
        send(w_hbm.at[part], bw.at[m, part], bs.at[1, r], br.at[m, r], core_mate)

    for i in range(NH):
        k = (head + i) % NH
        if i == 0:
            local[2].wait()
        else:
            arrived(s1.at[k], p1r.at[k], at_head(k))

        @pl.when(k == z)
        def _():
            pltpu.make_async_copy(s1.at[k], a.at[head, z], loc.at[5]).start()

        @pl.when(k != z)
        def _():
            remote(s1.at[k], a.at[head, z], p2s.at[k], p2r.at[z], at_z(k)).start()

    @pl.when(z == NZ - 1)
    def _():
        for i in range(NZ - 1):
            remote(k_hbm, kv.at[0, 2 * m + 1], pxs.at[0, i], pxr.at[0], at_z(i)).start()
            remote(v_hbm, kv.at[1, 2 * m + 1], pxs.at[1, i], pxr.at[1], at_z(i)).start()

    local[0].wait()
    local[1].wait()
    for i in range(1, GROUP):
        mm = (m + i) % GROUP
        for c in range(2):
            send(kv.at[c, 2 * m], kv.at[c, 2 * m], kvs.at[c, 0, i], kvr.at[c, 2 * m], at_m(mm))

    shape = bias.shape
    row = lax.broadcasted_iota(jnp.int32, shape, 0)
    col = lax.broadcasted_iota(jnp.int32, shape, 1)
    key_block = col // (2 * DH)
    in_prefix = (col // DH) % 2
    within = col % DH
    own_kind = jnp.where(z == NZ - 1, 1, 0)
    root = jnp.where(z == NZ - 1, GROUP, parent_ref[z * GROUP + GROUP - 1] - (NZ - 1) * GROUP)
    own_part = (in_prefix == own_kind) & (
        (key_block > m) | ((key_block == m) & (within <= row))
    )
    allowed = own_part | ((in_prefix == 1) & (key_block >= root))
    bias[...] = jnp.where(allowed, 0.0, -1e30)
    local[3].wait()
    for h in range(HPG):
        cols = pl.ds(h * DH, DH)
        qt[:, cols] = q_v[:, cols].astype(F32).T.astype(BF16)

    for i in range(1, NZ):
        zz = (z + i) % NZ
        arrived(a.at[head, zz], p2r.at[zz], at_z(zz))
    pltpu.make_async_copy(s1.at[0], a.at[head, z], loc.at[5]).wait()

    def x_at(dx):
        return 2 * ((x + dx) % 4) + yh

    h_y = 2 * x + 1 - yh
    send(a.at[head], a.at[head], ags.at[0], agr.at[head], at_head(x_at(1)))
    send(a.at[head], a.at[head], ags.at[1], agr.at[head], at_head(x_at(3)))
    send(a.at[head], a.at[head], ags.at[2], agr.at[head], at_head(h_y))
    send(a.at[head], a.at[head], ags.at[3], agr.at[head], at_head(x_at(2)))

    def forward_head(h, carry):
        cols = pl.ds(pl.multiple_of(h * DH, DH), DH)
        keys = kv[0].reshape(2 * GROUP * DH, DH)
        s = dot_nt(q_v[:, cols], keys) * scale + bias[...]
        w = jnp.exp(s - jnp.max(s, axis=1, keepdims=True))
        p = w * (1.0 / jnp.sum(w, axis=1, keepdims=True))
        pf[cols, :] = p
        plow[cols, :] = p.astype(BF16)
        return carry

    for r in range(2):
        part = pl.ds(r * half, half)
        arrived(bw.at[m_side, part], br.at[m_side, r], core_mate)
        send(bw.at[m_side, part], bw.at[m_side, part], bs.at[2, r], br.at[m_side, r], core_mate)

    @pl.when(z == NZ - 1)
    def _():
        for c in range(2):
            pltpu.make_async_copy(kv.at[c, 2 * m], kv.at[c, 2 * m + 1], loc.at[6 + c]).start()
        for c in range(2):
            pltpu.make_async_copy(kv.at[c, 2 * m], kv.at[c, 2 * m + 1], loc.at[6 + c]).wait()

    @pl.when(z != NZ - 1)
    def _():
        for c in range(2):
            arrived(kv.at[c, 2 * m + 1], pxr.at[c], at_z(0))

    for i in range(1, GROUP):
        mm = (m + i) % GROUP
        for c in range(2):
            send(kv.at[c, 2 * m + 1], kv.at[c, 2 * m + 1], kvs.at[c, 1, i], kvr.at[c, 2 * m + 1], at_m(mm))

    local[4].wait()
    for r in range(2):
        part = pl.ds(r * half, half)
        arrived(bw.at[m_core, part], br.at[m_core, r], core_mate)
        arrived(bw.at[m_far, part], br.at[m_far, r], core_mate)

    up = at_z((z + 1) % NZ)
    down = at_z((z + NZ - 1) % NZ)
    width = s1.shape[2]
    steps = NZ // 2
    side = (pl.ds(0, width // 2), pl.ds(width // 2, width // 2))

    def head_of(j):
        dx = 0
        dy = 0
        for at, (vx, vy) in enumerate([(0, 0), (1, 0), (3, 0), (0, 1), (2, 0), (1, 1), (3, 1), (2, 1)]):
            hit = jnp.where(j == at, 1, 0)
            dx = dx + vx * hit
            dy = dy + vy * hit
        return 2 * ((x + dx) % 4) + (yh + dy) % 2

    def hop(j, d, s):
        where = (slice(None), side[d]) if s == 0 else (slice(None), slice(None))
        return remote(
            sp.at[(j, d, s) + where], rp.at[(j, d, s) + where], rss.at[j, d, s], rsr.at[j, d, s],
            up if d == 0 else down,
        )

    def slot(t, carry):
        for s in range(steps, 0, -1):
            j = t - SKEW * s

            @pl.when((j >= 0) & (j < NH))
            def _():
                for d in range(2):
                    hop(j, d, s - 1).wait_recv()
                    if s < steps:
                        dest = (z + steps - s) % NZ if d == 0 else (z + steps + s) % NZ
                        mine = pl.ds(pl.multiple_of(dest * ROWS, ROWS), ROWS)
                        if s == 1:
                            other = side[1 - d]
                            sp[j, d, s, :, side[d]] = (
                                cb[j, mine, side[d]] + rp[j, d, 0, :, side[d]].astype(F32)
                            ).astype(BF16)
                            sp[j, d, s, :, other] = cb[j, mine, other].astype(BF16)
                        else:
                            sp[j, d, s] = (cb[j, mine, :] + rp[j, d, s - 1].astype(F32)).astype(BF16)
                        hop(j, d, s).start()
                if s == steps:
                    mine = pl.ds(pl.multiple_of(z * ROWS, ROWS), ROWS)
                    total = cb[j, mine, :] + rp[j, 0, s - 1].astype(F32) + rp[j, 1, s - 1].astype(F32)
                    place = pl.multiple_of(head_of(j) * ROWS, ROWS)
                    ga[pl.ds(place, ROWS), :] = total.astype(BF16)

        @pl.when(t < NH)
        def _():
            h = head_of(t)

            @pl.when(t > 0)
            def _():
                arrived(a.at[h], agr.at[h], at_head(h_y))

            @pl.when(t == 3)
            def _():
                remote(a.at[h], a.at[h], ags.at[4], agr.at[h], at_head(x_at(1))).start()
                remote(a.at[h], a.at[h], ags.at[5], agr.at[h], at_head(x_at(3))).start()

            @pl.when(t == 4)
            def _():
                remote(a.at[h], a.at[h], ags.at[6], agr.at[h], at_head(h_y)).start()

            wide = bw.shape[2]
            for n in range(width // wide):
                cols = pl.ds(n * wide, wide)
                acc = None
                for b in range(GROUP):
                    rows = a[h, :, :, pl.ds(b * wide, wide)].reshape(NZ * ROWS, wide)
                    term = dot_nt(rows, bw[b, cols, :])
                    acc = term if acc is None else acc + term
                cb[t, :, cols] = acc
            far = pl.ds(pl.multiple_of(((z + steps) % NZ) * ROWS, ROWS), ROWS)
            for d in range(2):
                sp[t, d, 0, :, side[d]] = cb[t, far, side[d]].astype(BF16)
                hop(t, d, 0).start()

        @pl.when(t == NH - 1)
        def _():
            for c in range(2):
                for i in range(1, GROUP):
                    mm = (m + i) % GROUP
                    for e in range(2):
                        arrived(kv.at[c, 2 * mm + e], kvr.at[c, 2 * mm + e], at_m(mm))

        @pl.when((t >= NH - 1) & (t < NH - 1 + HPG))
        def _():
            forward_head(t - (NH - 1), carry)

        return carry

    lax.fori_loop(0, NH + SKEW * steps, slot, 0)

    mates = [(m + i) % GROUP for i in range(1, GROUP)]

    def spread(c, scaled):
        for b in range(2 * GROUP):
            dsend[c, b] = (dt[c, :, pl.ds(b * DH, DH)] * scaled).astype(BF16)
        share(c, 1)

    def share(c, e):
        for i, mm in enumerate(mates):
            send(dsend.at[c, 2 * mm + e], r1.at[c, m, e], d1s.at[c, e, i], d1r.at[c, e, m], at_m(mm))

    for h in range(HPG):
        cols = pl.ds(h * DH, DH)
        gat[:, cols] = ga[:, cols].astype(F32).T.astype(BF16)
    dt[0] = dot_nn(gat[...], plow[...])
    spread(0, 1.0)

    def backward_head(h, carry):
        cols = pl.ds(pl.multiple_of(h * DH, DH), DH)
        values = kv[1].reshape(2 * GROUP * DH, DH)
        dprob = dot_nt(ga[:, cols], values)
        p = pf[cols, :]
        delta = jnp.sum(p * dprob, axis=1, keepdims=True)
        ds[cols, :] = (p * (dprob - delta)).astype(BF16)
        return carry

    lax.fori_loop(0, HPG, backward_head, 0)
    dt[1] = dot_nn(qt[...], ds[...])
    spread(1, scale)
    share(0, 0)
    share(1, 0)

    def query_head(h, carry):
        cols = pl.ds(pl.multiple_of(h * DH, DH), DH)
        keys = kv[0].reshape(2 * GROUP * DH, DH)
        dq_ref[:, cols] = (dot_nn(ds[cols, :], keys) * scale).astype(BF16)
        return carry

    lax.fori_loop(0, HPG, query_head, 0)

    last = at_z(NZ - 1)

    def collect(c, e):
        cols = pl.ds(pl.multiple_of((2 * m + e) * DH, DH), DH)
        total = dt[c, :, cols] * (scale if c else 1.0)
        for mm in mates:
            arrived(r1.at[c, mm, e], d1r.at[c, e, mm], at_m(mm))
            total = total + r1[c, mm, e].astype(F32)
        fin[c, e] = total

    for c in range(2):
        collect(c, 1)

        @pl.when(z != NZ - 1)
        def _():
            psend[c] = fin[c, 1].astype(BF16)
            remote(psend.at[c], r2.at[c, z], d2s.at[c], d2r.at[c, z], last).start()

    for c in range(2):
        collect(c, 0)

    for c in range(2):
        @pl.when(z == NZ - 1)
        def _():
            total = fin[c, 0] + fin[c, 1]
            for i in range(1, NZ):
                zz = NZ - 1 - i
                arrived(r2.at[c, zz], d2r.at[c, zz], at_z(zz))
                total = total + r2[c, zz].astype(F32)
            fin[c, 0] = total

        out = dk_ref if c else dv_ref
        out[...] = fin[c, 0].T.astype(BF16)

    for copy in sends:
        copy.wait_send()
    for k in range(NH):
        @pl.when(k != z)
        def _():
            remote(s1.at[k], a.at[head, z], p2s.at[k], p2r.at[z], up).wait_send()

    for i in range(4, 7):
        remote(a.at[head], a.at[head], ags.at[i], agr.at[head], up).wait_send()

    @pl.when(z == NZ - 1)
    def _():
        for i in range(NZ - 1):
            remote(k_hbm, kv.at[0, 2 * m + 1], pxs.at[0, i], pxr.at[0], up).wait_send()
            remote(v_hbm, kv.at[1, 2 * m + 1], pxs.at[1, i], pxr.at[1], up).wait_send()

    @pl.when(z != NZ - 1)
    def _():
        for c in range(2):
            remote(psend.at[c], r2.at[c, z], d2s.at[c], d2r.at[c, z], up).wait_send()

    def drain(j, carry):
        for d in range(2):
            for s in range(steps):
                hop(j, d, s).wait_send()
        return carry

    lax.fori_loop(0, NH, drain, 0)


def per_device(query, key_in, value, grad_y, w_out, parent):
    tokens, width = query.shape
    keys = 2 * GROUP * DH
    dma = pltpu.SemaphoreType.DMA
    anywhere = pl.BlockSpec(memory_space=pl.ANY)
    vmem = pl.BlockSpec(memory_space=pltpu.VMEM)
    return pl.pallas_call(
        kernel,
        out_shape=(
            jax.ShapeDtypeStruct(query.shape, BF16),
            jax.ShapeDtypeStruct(key_in.shape, BF16),
            jax.ShapeDtypeStruct(value.shape, BF16),
        ),
        in_specs=[anywhere] * 5 + [pl.BlockSpec(memory_space=pltpu.SMEM)],
        out_specs=(vmem, vmem, vmem),
        scratch_shapes=[
            pltpu.VMEM((tokens, width), BF16),
            pltpu.VMEM((2, 2 * GROUP, DH, DH), BF16),
            pltpu.VMEM((NH, ROWS, width), BF16),
            pltpu.VMEM((NH, NZ, ROWS, width), BF16),
            pltpu.VMEM((GROUP,) + w_out.shape, BF16),
            pltpu.VMEM((NH, tokens, width), F32),
            pltpu.VMEM((NH, 2, NZ // 2, ROWS, width), BF16),
            pltpu.VMEM((NH, 2, NZ // 2, ROWS, width), BF16),
            pltpu.VMEM((tokens, width), BF16),
            pltpu.VMEM((tokens, width), BF16),
            pltpu.VMEM((tokens, width), BF16),
            pltpu.VMEM((tokens, keys), F32),
            pltpu.VMEM((width, keys), F32),
            pltpu.VMEM((width, keys), BF16),
            pltpu.VMEM((width, keys), BF16),
            pltpu.VMEM((2, DH, keys), F32),
            pltpu.VMEM((2, 2 * GROUP, DH, DH), BF16),
            pltpu.VMEM((2, GROUP, 2, DH, DH), BF16),
            pltpu.VMEM((2, DH, DH), BF16),
            pltpu.VMEM((2, NZ, DH, DH), BF16),
            pltpu.VMEM((2, 2, DH, DH), F32),
            dma((8,)),
            dma((NH,)), dma((NH,)),
            dma((NH,)), dma((NZ,)),
            dma((7,)), dma((NH,)),
            dma((3, 2)), dma((GROUP, 2)),
            dma((2, 2, GROUP)), dma((2, 2 * GROUP)),
            dma((2, NZ)), dma((2,)),
            dma((NH, 2, NZ // 2)), dma((NH, 2, NZ // 2)),
            dma((2, 2, GROUP)), dma((2, 2, GROUP)),
            dma((2,)), dma((2, NZ)),
        ],
        compiler_params=pltpu.CompilerParams(
            collective_id=0, has_side_effects=True, vmem_limit_bytes=60 * 1024 * 1024
        ),
        name="tree_attention_backward",
    )(query, key_in, value, grad_y, w_out, parent)


def solution(mesh):
    placed = (
        P("ctx", "head"),
        P("ctx", "head"),
        P("ctx", "head"),
        P("ctx", "head"),
        P("head", "ctx"),
        P(),
    )
    return jax.shard_map(
        per_device,
        mesh=mesh,
        in_specs=placed,
        out_specs=(P("ctx", "head"), P("ctx", "head"), P("ctx", "head")),
        check_vma=False,
    )
```
